256 devices in a mesh: seq: 16 (over z, core), head: 16 (over y, x).
Axes of the slice: x: 4, y: 4, z: 8, core: 2. Of those that a mesh axis runs over, the one named last changes fastest.
Arguments:
- queries: bfloat16 [6144, 16384], P('seq', 'head'), may hold values from -5 to 5
- keys: bfloat16 [6144, 1024], P('seq', 'head'), may hold values from -5 to 5
- values: bfloat16 [6144, 1024], P('seq', 'head'), may hold values from -6 to 6
- feat_q: bfloat16 [128, 128, 128], P('head'), may hold values from -0.5 to 0.5
- feat_k: bfloat16 [128, 128, 128], P('head'), may hold values from -0.5 to 0.5
Outputs:
- grad_feat_q: float32 [128, 128, 128], P('head')
- grad_feat_k: float32 [128, 128, 128], P('head')
The draws below stay inside these ranges and needn't reach their ends.
All inputs are finite; a program needn't handle non-finite values.
Results may differ from the reference program's by a relative error of at most 0.02.
Values may be sent and summed in bfloat16 or wider, within the bound.
A program may use at most 128 MiB of HBM per device.

```python
import math
import jax
import jax.numpy as jnp
from jax import lax

HEADS = 128
KV_HEADS = 8
HD = 128
FD = 128
TOK_DEV = 384
TOKENS = 6144


def drawn_inputs(base_key):
    query_seed, key_seed = jax.random.split(jax.random.fold_in(base_key, 1234), 2)
    queries = jax.random.truncated_normal(query_seed, -5.0, 5.0, (TOKENS, HEADS * HD), jnp.float32)
    keys = jax.random.truncated_normal(key_seed, -5.0, 5.0, (TOKENS, KV_HEADS * HD), jnp.float32)
    return (queries, keys)


def draw_queries(key, part):
    return drawn_inputs(key)[0].astype(jnp.bfloat16)


def draw_keys(key, part):
    return drawn_inputs(key)[1].astype(jnp.bfloat16)


def block_scale(stream_key, extent, cuts, low, largest):
    factor_of = 1.0
    for position, parts in cuts:
        steps = jax.random.uniform(jax.random.fold_in(jax.random.fold_in(stream_key, 6), position), (parts,), jnp.float32, low / len(cuts), largest / len(cuts))
        factor_of = factor_of * jnp.repeat(jnp.exp(steps), extent[position] // parts).reshape((-1,) + (1,) * (len(extent) - 1 - position))
    return factor_of


def bell_draw(own_key, dims, scale, limit, shards=(), kind=jnp.bfloat16):
    values = scale * jax.random.normal(own_key, dims, jnp.float32)
    if shards:
        values = values * block_scale(own_key, dims, shards, -0.22, 0.18)
    return jnp.clip(values, -limit, limit).astype(kind)


def setup_inputs(seed: int = 0) -> dict:
    key_of = jax.random.split(jax.random.key(seed), 6)
    return {
        "queries": draw_queries(jax.random.fold_in(key_of[5], 71), 0),
        "keys": draw_keys(jax.random.fold_in(key_of[5], 71), 0),
        "values": bell_draw(key_of[2], (TOKENS, KV_HEADS * HD), 1.0, 6.0, ((0, 16), (1, 16))),
        "feat_q": bell_draw(key_of[3], (HEADS, HD, FD), HD ** -0.5, 0.5, ((0, 16),)),
        "feat_k": bell_draw(key_of[4], (HEADS, HD, FD), HD ** -0.5, 0.5, ((0, 16),)),
    }


HIGHEST_MODE = lax.Precision.HIGHEST
MASKED_SCORE = -1e30


def rounded_wide(entries):
    return lax.optimization_barrier(entries.astype(jnp.bfloat16)).astype(jnp.float32)


def exclusive_sum(stacked):
    totals = jnp.cumsum(stacked, axis=0)
    return jnp.concatenate([jnp.zeros_like(stacked[:1]), totals[:-1]], axis=0)


def teacher_group(query_heads, key_rows, value_rows):
    block_rows = math.gcd(TOKENS, 512)
    score_scale = HD ** -0.5
    pieces = []
    for block_index in range(TOKENS // block_rows):
        finish = (block_index + 1) * block_rows
        query_block = query_heads[:, block_index * block_rows:finish].astype(jnp.float32)
        scores = jnp.einsum("jrd,kd->jrk", query_block, key_rows[:finish].astype(jnp.float32)) * score_scale
        query_pos = block_index * block_rows + jnp.arange(block_rows, dtype=jnp.int32)
        key_pos = jnp.arange(finish, dtype=jnp.int32)
        allowed = (key_pos[None, :] <= query_pos[:, None])[None]
        row_peak = jnp.max(jnp.where(allowed, scores, MASKED_SCORE), axis=-1)
        weights = jnp.exp(jnp.where(allowed, scores - row_peak[..., None], MASKED_SCORE))
        row_total = jnp.sum(weights, axis=-1)
        mixture = jnp.einsum("jrk,kd->jrd", rounded_wide(weights), value_rows[:finish].astype(jnp.float32))
        pieces.append((mixture / row_total[..., None]).astype(jnp.bfloat16))
    return jnp.concatenate(pieces, axis=1)


def student_group(query_heads, key_rows, value_rows, teacher_out, weight_query, weight_key):
    group_size = query_heads.shape[0]
    block_count = TOKENS // TOK_DEV
    query_wide = query_heads.astype(jnp.float32)
    key_wide = key_rows.astype(jnp.float32)
    query_pre = jnp.einsum("jtd,jdf->jtf", query_wide, weight_query.astype(jnp.float32))
    key_pre = jnp.einsum("td,jdf->jtf", key_wide, weight_key.astype(jnp.float32))
    query_feat = rounded_wide(jax.nn.softplus(query_pre))
    key_feat = rounded_wide(jax.nn.softplus(key_pre))

    def split_blocks(entries):
        return entries.reshape(group_size, block_count, TOK_DEV, -1).transpose(1, 0, 2, 3)

    query_blocks = split_blocks(query_feat)
    key_blocks = split_blocks(key_feat)
    value_blocks = value_rows.astype(jnp.float32).reshape(block_count, TOK_DEV, -1)
    teacher_blocks = split_blocks(teacher_out.astype(jnp.float32))
    block_state = jnp.einsum("njbf,nbd->njfd", key_blocks, value_blocks)
    block_norm = jnp.sum(key_blocks, axis=2)
    before_state = exclusive_sum(block_state)
    before_norm = exclusive_sum(block_norm)
    causal = jnp.arange(TOK_DEV)[:, None] >= jnp.arange(TOK_DEV)[None, :]

    def forward_one(items):
        query_part, key_part, value_part, teacher_part, state_part, norm_part = items
        affinity = jnp.where(causal, jnp.einsum("jrf,jsf->jrs", query_part, key_part), 0.0)
        local_mix = jnp.einsum("jrs,sd->jrd", rounded_wide(affinity), value_part)
        numerator = jnp.einsum("jrf,jfd->jrd", query_part, state_part, precision=HIGHEST_MODE) + local_mix
        denominator = jnp.einsum("jrf,jf->jr", query_part, norm_part, precision=HIGHEST_MODE) + jnp.sum(affinity, axis=-1)
        student = numerator / denominator[..., None]
        grad_out = 2.0 * (student - teacher_part) / TOKENS
        grad_numer = grad_out / denominator[..., None]
        grad_denom = -jnp.sum(grad_out * student, axis=-1) / denominator
        back_state = jnp.einsum("jrf,jrd->jfd", query_part, grad_numer, precision=HIGHEST_MODE)
        back_norm = jnp.einsum("jrf,jr->jf", query_part, grad_denom, precision=HIGHEST_MODE)
        return grad_numer, grad_denom, back_state, back_norm

    grad_numer, grad_denom, back_state, back_norm = lax.map(
        forward_one, (query_blocks, key_blocks, value_blocks, teacher_blocks, before_state, before_norm))
    after_state = exclusive_sum(back_state[::-1])[::-1]
    after_norm = exclusive_sum(back_norm[::-1])[::-1]

    def backward_one(items):
        (query_part, key_part, value_part, qpre_part, kpre_part, qin_part, kin_part,
         state_part, norm_part, later_state, later_norm, numer_part, denom_part) = items
        grad_aff = jnp.einsum("jrd,sd->jrs", numer_part, value_part, precision=HIGHEST_MODE) + denom_part[..., None]
        grad_aff = jnp.where(causal, grad_aff, 0.0)
        grad_qfeat = (jnp.einsum("jrd,jfd->jrf", numer_part, state_part, precision=HIGHEST_MODE)
                      + denom_part[..., None] * norm_part[:, None, :]
                      + jnp.einsum("jrs,jsf->jrf", grad_aff, key_part, precision=HIGHEST_MODE))
        grad_kfeat = (jnp.einsum("sd,jfd->jsf", value_part, later_state, precision=HIGHEST_MODE)
                      + later_norm[:, None, :]
                      + jnp.einsum("jrs,jrf->jsf", grad_aff, query_part, precision=HIGHEST_MODE))
        grad_wq = jnp.einsum("jrd,jrf->jdf", qin_part, grad_qfeat * jax.nn.sigmoid(qpre_part), precision=HIGHEST_MODE)
        grad_wk = jnp.einsum("rd,jrf->jdf", kin_part, grad_kfeat * jax.nn.sigmoid(kpre_part), precision=HIGHEST_MODE)
        return grad_wq, grad_wk

    grad_wq, grad_wk = lax.map(backward_one, (
        query_blocks, key_blocks, value_blocks, split_blocks(query_pre), split_blocks(key_pre),
        split_blocks(query_wide), key_wide.reshape(block_count, TOK_DEV, -1),
        before_state, before_norm, after_state, after_norm, grad_numer, grad_denom))
    return jnp.sum(grad_wq, axis=0), jnp.sum(grad_wk, axis=0)


def reference(queries, keys, values, feat_q, feat_k):
    group_size = HEADS // KV_HEADS
    query_groups = queries.reshape(TOKENS, KV_HEADS, group_size, HD).transpose(1, 2, 0, 3)
    key_groups = keys.reshape(TOKENS, KV_HEADS, HD).transpose(1, 0, 2)
    value_groups = values.reshape(TOKENS, KV_HEADS, HD).transpose(1, 0, 2)
    weight_query = feat_q.reshape(KV_HEADS, group_size, HD, FD)
    weight_key = feat_k.reshape(KV_HEADS, group_size, HD, FD)

    def one_group(items):
        query_heads, key_rows, value_rows, query_map, key_map = items
        teacher_out = teacher_group(query_heads, key_rows, value_rows)
        return student_group(query_heads, key_rows, value_rows, teacher_out, query_map, key_map)

    grad_q, grad_k = lax.map(one_group, (query_groups, key_groups, value_groups, weight_query, weight_key))
    return grad_q.reshape(HEADS, HD, FD), grad_k.reshape(HEADS, HD, FD)
```

```python
import jax
import jax.numpy as jnp
from jax import lax
from jax.experimental import pallas as pl
from jax.experimental.pallas import tpu as pltpu
from jax.sharding import PartitionSpec as P

BF = jnp.bfloat16
F32 = jnp.float32
R = 384
NB = 16
HD = 128
LOG2E = 1.4426950408889634


def nn(a, b):
    return lax.dot_general(a, b, (((1,), (0,)), ((), ())), preferred_element_type=F32)


def nt(a, b):
    return lax.dot_general(a, b, (((1,), (1,)), ((), ())), preferred_element_type=F32)


def split(x):
    hi = x.astype(BF)
    return hi, (x - hi.astype(F32)).astype(BF)


def soft(v):
    e = jnp.exp(-jnp.abs(v))
    feat = jnp.maximum(v, 0.0) + jnp.log1p(e)
    gate = jnp.where(v >= 0.0, 1.0, e) / (1.0 + e)
    return feat.astype(BF), gate


def prepare(kv, wkt, ks, vs, vts, kfs, sgs, bs, bst, bn):
    lane = lax.broadcasted_iota(jnp.int32, (R, HD), 1)
    ones = jnp.ones((R, HD), BF)

    def block(b, carry):
        st, stt, nm = carry
        x0 = kv[0, b].astype(F32)
        x1 = kv[1, b].astype(F32)
        k = jnp.where(lane < 64, x0, pltpu.roll(x1, 64, 1)).astype(BF)
        vf = jnp.where(lane < 64, pltpu.roll(x0, 64, 1), x1)
        v = vf.astype(BF)
        vt = vf.T.astype(BF)
        ks[b] = k
        vs[b] = v
        vts[b] = vt
        kf, sg = soft(nt(wkt, k))
        kfs[b] = kf
        sgs[b] = sg
        bs[b] = st
        bst[b] = stt
        bn[b] = nm
        return (st + nn(kf, v), stt + nt(vt, kf), nm + nn(kf, ones))

    zero = jnp.zeros((HD, HD), F32)
    lax.fori_loop(0, NB, block, (zero, zero, zero))


def attend(q, b, ks, vts):
    qs = (q.astype(F32) * (HD**-0.5 * LOG2E)).astype(BF)
    row = lax.broadcasted_iota(jnp.int32, (R, R), 0)
    col = lax.broadcasted_iota(jnp.int32, (R, R), 1)
    s = jnp.where(row <= col, nt(ks[b], qs), -1e30)
    m = jnp.max(s, axis=0, keepdims=True)
    p = jnp.exp2(s - m)
    l = jnp.sum(p, axis=0, keepdims=True)
    acc = nn(vts[b], p.astype(BF))

    def step(k, carry):
        m, l, acc = carry
        s = nt(ks[k], qs)
        mn = jnp.maximum(m, jnp.max(s, axis=0, keepdims=True))
        p = jnp.exp2(s - mn)
        a = jnp.exp2(m - mn)
        l = l * a + jnp.sum(p, axis=0, keepdims=True)
        acc = acc * a + nn(vts[k], p.astype(BF))
        return mn, l, acc

    m, l, acc = lax.fori_loop(0, b, step, (m, l, acc))
    return (acc / l).astype(BF).astype(F32)


def own_block(q, b, teacher, wqt, ks, vs, vts, kfs, bs, bst, bn, tokens):
    qf, sq = soft(nt(wqt, q))
    kf = kfs[b]
    row = lax.broadcasted_iota(jnp.int32, (R, R), 0)
    col = lax.broadcasted_iota(jnp.int32, (R, R), 1)
    keep = row <= col
    aff = jnp.where(keep, lax.dot_general(kf, qf, (((0,), (0,)), ((), ())), preferred_element_type=F32), 0.0)
    mix = nn(vts[b], aff.astype(BF))
    sh, sl = split(bst[b])
    num = nn(sh, qf) + nn(sl, qf) + mix
    norm = bn[b][:, :1]
    den = jnp.sum(norm * qf.astype(F32), axis=0, keepdims=True) + jnp.sum(aff, axis=0, keepdims=True)
    inv = 1.0 / den
    student = num * inv
    go = (student - teacher) * (2.0 / tokens)
    gn = go * inv
    gd = -jnp.sum(go * student, axis=0, keepdims=True) * inv
    gh, gl = split(gn)
    back = nt(qf, gh) + nt(qf, gl)
    backn = jnp.sum(qf.astype(F32) * gd, axis=1, keepdims=True)
    v = vs[b]
    ga = jnp.where(keep, nn(v, gh) + nn(v, gl) + gd, 0.0)
    gab = ga.astype(BF)
    bh, bl = split(bs[b])
    gqf = nn(bh, gh) + nn(bh, gl) + nn(bl, gh) + norm * gd + nn(kf, gab)
    gk = nt(qf, gab)
    th, tl = split(gqf * sq)
    return nn(th, q) + nn(tl, q), back, backn, gk


def compute(c, qa, wqt, wkt, kv, ks, vs, vts, kfs, sgs, bs, bst, bn, gks, bks, bkn):
    tokens = NB * R
    prepare(kv, wkt, ks, vs, vts, kfs, sgs, bs, bst, bn)
    zero = jnp.zeros((HD, HD), F32)

    def slot(j, gwq):
        o = (c + j) % 2
        b = 2 * j + o
        q = qa[j]
        teacher = attend(q, b, ks, vts)
        g, back, backn, gk = own_block(q, b, teacher, wqt, ks, vs, vts, kfs, bs, bst, bn, tokens)
        gks[b] = gk
        gks[2 * j + 1 - o] = jnp.zeros((HD, R), F32)
        bks[b] = back
        bks[2 * j + 1 - o] = zero
        bkn[b] = jnp.broadcast_to(backn, (HD, HD))
        bkn[2 * j + 1 - o] = zero
        return gwq + g

    gwq = lax.fori_loop(0, NB // 2, slot, zero)

    def late(i, carry):
        st, nm, gwk = carry
        b = NB - 1 - i
        sh, sl = split(st)
        vt = vts[b]
        gk = nn(sh, vt) + nn(sl, vt) + nm[:, :1] + gks[b]
        th, tl = split(gk * sgs[b])
        k = ks[b]
        return (st + bks[b], nm + bkn[b], gwk + nn(th, k) + nn(tl, k))

    _, _, gwk = lax.fori_loop(0, NB, late, (zero, zero, zero))
    return gwq, gwk


def scratch():
    return [
        pltpu.VMEM((NB, R, HD), BF),
        pltpu.VMEM((NB, R, HD), BF),
        pltpu.VMEM((NB, HD, R), BF),
        pltpu.VMEM((NB, HD, R), BF),
        pltpu.VMEM((NB, HD, R), F32),
        pltpu.VMEM((NB, HD, HD), F32),
        pltpu.VMEM((NB, HD, HD), F32),
        pltpu.VMEM((NB, HD, HD), F32),
        pltpu.VMEM((NB, HD, R), F32),
        pltpu.VMEM((NB, HD, HD), F32),
        pltpu.VMEM((NB, HD, HD), F32),
    ]


ORDER = ((0, 1), (1, 1), (0, 2), (1, 2), (0, 3), (1, 3), (0, 4))
FAR = (1, 7, 2, 6, 3, 5, 4)
MESH_ID = pl.DeviceIdType.MESH


def place():
    s = lax.axis_index("seq")
    return s, lax.axis_index("head"), s // 2, s % 2


def greet(s, p, with_pair):
    barrier = pltpu.get_barrier_semaphore()
    for d in range(1, NB):
        pl.semaphore_signal(barrier, inc=1, device_id=((s + d) % NB, p), device_id_type=MESH_ID)
    if with_pair:
        pl.semaphore_signal(barrier, inc=1, device_id=(s, p + 1 - 2 * (p % 2)), device_id_type=MESH_ID)
    pl.semaphore_wait(barrier, NB - 1 + int(with_pair))


def gather_kernel(q, kvin, qa, kv, ring_s, ring_r, pair_s, pair_r, core_s, core_r, q_s, q_r, own_sem):
    s, p, z, c = place()
    u = p % 2
    pair = (s, p + 1 - 2 * u)
    core = (2 * z + 1 - c, p)

    def remote(src, dst, ss, rs, to):
        return pltpu.make_async_remote_copy(
            src_ref=src, dst_ref=dst, send_sem=ss, recv_sem=rs, device_id=to, device_id_type=MESH_ID
        )

    greet(s, p, True)
    started = []

    def go(copy):
        copy.start()
        started.append(copy)

    def at(half, zi, par):
        return kv.at[half, 2 * zi + par]

    def ring(way, step, src, zi):
        to = (2 * ((z + (1 if way == 0 else 7)) % 8) + c, p)
        return remote(src, at(u, zi, c), ring_s.at[way, step], ring_r.at[way, step], to)

    keep = pltpu.make_async_copy(kvin, at(u, z, c), own_sem.at[0])
    keep.start()
    go(ring(0, 0, kvin, z))
    go(ring(1, 0, kvin, z))
    go(remote(kvin, at(u, z, c), pair_s.at[0], pair_r.at[0], pair))
    go(remote(kvin, at(u, z, c), core_s.at[0, 0], core_r.at[0, 0], core))

    zs = [z]
    for i, (way, hop) in enumerate(ORDER, 1):
        zi = (z + (8 - hop if way == 0 else hop)) % 8
        zs.append(zi)
        got = at(u, zi, c)
        ring(way, hop - 1, got, zi).wait_recv()
        if hop < (4 if way == 0 else 3):
            go(ring(way, hop, got, zi))
        go(remote(got, got, pair_s.at[i], pair_r.at[i], pair))
        go(remote(got, got, core_s.at[0, i], core_r.at[0, i], core))
        if i == 5:
            for d in FAR:
                h = (z + d) % 8
                go(
                    remote(
                        q.at[:, pl.ds(pl.multiple_of(h * HD, HD), HD)],
                        qa.at[z],
                        q_s.at[d],
                        q_r.at[d],
                        (2 * h + (c + z) % 2, p),
                    )
                )
    mine = q.at[:, pl.ds(pl.multiple_of(z * HD, HD), HD)]

    @pl.when(z % 2 == 0)
    def _():
        stay = pltpu.make_async_copy(mine, qa.at[z], own_sem.at[1])
        stay.start()
        stay.wait()

    @pl.when(z % 2 == 1)
    def _():
        cross = remote(mine, qa.at[z], q_s.at[0], q_r.at[0], core)
        cross.start()
        cross.wait()

    for i, zi in enumerate(zs):
        got = at(1 - u, zi, c)
        remote(got, got, pair_s.at[i], pair_r.at[i], pair).wait_recv()
        go(remote(got, got, core_s.at[1, i], core_r.at[1, i], core))
    for i, zi in enumerate(zs):
        for j, half in enumerate((u, 1 - u)):
            got = at(half, zi, 1 - c)
            remote(got, got, core_s.at[j, i], core_r.at[j, i], core).wait_recv()
    for d in FAR:
        got = qa.at[(z + 8 - d) % 8]
        remote(got, got, q_s.at[d], q_r.at[d], core).wait_recv()
    keep.wait()
    for copy in started:
        copy.wait_send()


def gather_call(queries, kvin):
    dma = pltpu.SemaphoreType.DMA
    return pl.pallas_call(
        gather_kernel,
        out_shape=(
            jax.ShapeDtypeStruct((8, R, HD), BF),
            jax.ShapeDtypeStruct((2, NB, R, HD), BF),
        ),
        in_specs=[pl.BlockSpec(memory_space=pltpu.VMEM)] * 2,
        out_specs=[pl.BlockSpec(memory_space=pl.ANY)] * 2,
        scratch_shapes=[
            dma((2, 4)), dma((2, 4)), dma((8,)), dma((8,)), dma((2, 8)), dma((2, 8)), dma((8,)), dma((8,)), dma((2,)),
        ],
        compiler_params=pltpu.CompilerParams(collective_id=0, has_side_effects=True),
    )(queries, kvin)


def spread_kernel(part, gq, gk, other, mine, theirs, swap_s, swap_r, far_s, far_r, core_s, core_r):
    s, p, z, c = place()
    core = (2 * z + 1 - c, p)

    def remote(src, dst, ss, rs, to):
        return pltpu.make_async_remote_copy(
            src_ref=src, dst_ref=dst, send_sem=ss, recv_sem=rs, device_id=to, device_id_type=MESH_ID
        )

    greet(s, p, False)
    swap = remote(part.at[1 - c], other, swap_s, swap_r, core)
    swap.start()
    swap.wait()
    mine[z] = (part[c] + other[...]).astype(BF)
    started = []
    for d in FAR:
        copy = remote(mine.at[z], mine.at[z], far_s.at[d], far_r.at[d], (2 * ((z + d) % 8) + c, p))
        copy.start()
        started.append(copy)
    for d in (0,) + FAR:
        zi = (z + 8 - d) % 8
        got = mine.at[zi]
        if d:
            remote(got, got, far_s.at[d], far_r.at[d], core).wait_recv()
        copy = remote(got, theirs.at[zi], core_s.at[d], core_r.at[d], core)
        copy.start()
        started.append(copy)
    for d in range(8):
        got = theirs.at[(z + 8 - d) % 8]
        remote(got, got, core_s.at[d], core_r.at[d], core).wait_recv()
    for copy in started:
        copy.wait_send()
    first = c == 0
    for h in range(8):
        a, b = mine[h].astype(F32), theirs[h].astype(F32)
        gq[h] = jnp.where(first, a, b)
        gk[h] = jnp.where(first, b, a)


def spread_call(part):
    dma = pltpu.SemaphoreType.DMA
    return pl.pallas_call(
        spread_kernel,
        out_shape=(jax.ShapeDtypeStruct((8, HD, HD), F32),) * 2,
        in_specs=[pl.BlockSpec(memory_space=pltpu.VMEM)],
        out_specs=[pl.BlockSpec(memory_space=pltpu.VMEM)] * 2,
        scratch_shapes=[
            pltpu.VMEM((HD, HD), F32), pltpu.VMEM((8, HD, HD), BF), pltpu.VMEM((8, HD, HD), BF),
            dma, dma, dma((8,)), dma((8,)), dma((8,)), dma((8,)),
        ],
        compiler_params=pltpu.CompilerParams(collective_id=1, has_side_effects=True),
    )(part)


def local_kernel(qa, kv, wq, wk, out, *scr):
    s = lax.axis_index("seq")
    z, c = s // 2, s % 2
    wqt = wq[z].astype(F32).T.astype(BF)
    wkt = wk[z].astype(F32).T.astype(BF)
    gwq, gwk = compute(c, qa, wqt, wkt, kv, *scr)
    out[0] = gwq.T
    out[1] = gwk.T


def local_call(qa, kv, wq, wk):
    return pl.pallas_call(
        local_kernel,
        out_shape=jax.ShapeDtypeStruct((2, HD, HD), F32),
        in_specs=[pl.BlockSpec(memory_space=pltpu.VMEM)] * 4,
        out_specs=pl.BlockSpec(memory_space=pltpu.VMEM),
        scratch_shapes=scratch(),
        compiler_params=pltpu.CompilerParams(vmem_limit_bytes=60000 * 1024),
    )(qa, kv, wq, wk)


def body(queries, keys, values, feat_q, feat_k):
    qa, kv = gather_call(queries, jnp.concatenate((keys, values), axis=1))
    return spread_call(local_call(qa, kv, feat_q, feat_k))


def solution(mesh):
    return jax.shard_map(
        body,
        mesh=mesh,
        in_specs=(P("seq", "head"), P("seq", "head"), P("seq", "head"), P("head", None, None), P("head", None, None)),
        out_specs=(P("head", None, None), P("head", None, None)),
        check_vma=False,
    )
```

```python
import jax
import jax.numpy as jnp
from jax import lax
from jax.experimental import pallas as pl
from jax.experimental.pallas import tpu as pltpu
from jax.sharding import PartitionSpec as P

BF = jnp.bfloat16
F32 = jnp.float32
R = 384
NB = 16
HD = 128
LOG2E = 1.4426950408889634


def nn(a, b):
    return lax.dot_general(a, b, (((1,), (0,)), ((), ())), preferred_element_type=F32)


def nt(a, b):
    return lax.dot_general(a, b, (((1,), (1,)), ((), ())), preferred_element_type=F32)


def split(x):
    hi = x.astype(BF)
    return hi, (x - hi.astype(F32)).astype(BF)


def soft(v):
    e = jnp.exp(-jnp.abs(v))
    feat = jnp.maximum(v, 0.0) + jnp.log1p(e)
    gate = jnp.where(v >= 0.0, 1.0, e) / (1.0 + e)
    return feat.astype(BF), gate


MESH_ID = pl.DeviceIdType.MESH
NZ = NB // 2
G = 2
RG = R // G


def prepare_block(b, kv, wkt, ks, vs, vts, kfs, sgs, bs, bst, bn):
    lane = lax.broadcasted_iota(jnp.int32, (R, HD), 1)
    x0 = kv[0, b].astype(F32)
    x1 = kv[1, b].astype(F32)
    k = jnp.where(lane < 64, x0, pltpu.roll(x1, 64, 1)).astype(BF)
    vf = jnp.where(lane < 64, pltpu.roll(x0, 64, 1), x1)
    v = vf.astype(BF)
    vt = vf.T.astype(BF)
    ks[b] = k
    vs[b] = v
    vts[b] = vt
    kf, sg = soft(nt(wkt, k))
    kfs[b] = kf
    sgs[b] = sg
    bs[b] = nn(kf, v)
    bst[b] = nt(vt, kf)
    bn[b] = nn(kf, jnp.ones((R, HD), BF))


def prefix(bs, bst, bn):
    def step(b, carry):
        a, t, n = carry
        nxt = (a + bs[b], t + bst[b], n + bn[b])
        bs[b] = a
        bst[b] = t
        bn[b] = n
        return nxt

    zero = jnp.zeros((HD, HD), F32)
    lax.fori_loop(0, NB, step, (zero, zero, zero))


def attend(slot, pair, shift, qs, ks, vs, ms, ls, accs):
    k = ks[pl.ds(2 * pair, 2)].reshape(2 * R, HD)
    v = vs[pl.ds(2 * pair, 2)].reshape(2 * R, HD)
    scores = [nt(qs[slot, g * RG : (g + 1) * RG], k) for g in range(G)]
    for g in range(G):
        rows = slice(g * RG, (g + 1) * RG)
        s = scores[g]
        if shift is not None:
            dif = lax.broadcasted_iota(jnp.int32, s.shape, 1) - lax.broadcasted_iota(jnp.int32, s.shape, 0)
            s = jnp.where(dif <= shift + g * RG, s, -1e30)
        m = ms[slot, rows]
        mn = jnp.maximum(m, jnp.max(s, axis=1, keepdims=True))
        p = jnp.exp2(s - jnp.concatenate([mn] * (2 * R // HD), axis=1))
        a = jnp.exp2(m - mn)
        part = p[:, :HD]
        for t in range(1, 2 * R // HD):
            part = part + p[:, t * HD : (t + 1) * HD]
        ms[slot, rows] = mn
        ls[slot, rows] = ls[slot, rows] * a + part
        accs[slot, rows] = accs[slot, rows] * a + nn(p.astype(BF), v)


def own_block(q, b, teacher, wqt, ks, vs, vts, kfs, bs, bst, bn, tokens):
    qf, sq = soft(nt(wqt, q))
    kf = kfs[b]
    row = lax.broadcasted_iota(jnp.int32, (R, R), 0)
    col = lax.broadcasted_iota(jnp.int32, (R, R), 1)
    keep = row <= col
    aff = jnp.where(keep, lax.dot_general(kf, qf, (((0,), (0,)), ((), ())), preferred_element_type=F32), 0.0)
    mix = nn(vts[b], aff.astype(BF))
    sh, sl = split(bst[b])
    num = nn(sh, qf) + nn(sl, qf) + mix
    norm = bn[b][:, :1]
    den = jnp.sum(norm * qf.astype(F32), axis=0, keepdims=True) + jnp.sum(aff, axis=0, keepdims=True)
    inv = 1.0 / den
    student = num * inv
    go = (student - teacher) * (2.0 / tokens)
    gn = go * inv
    gd = -jnp.sum(go * student, axis=0, keepdims=True) * inv
    gh, gl = split(gn)
    back = nt(qf, gh) + nt(qf, gl)
    backn = jnp.sum(qf.astype(F32) * gd, axis=1, keepdims=True)
    v = vs[b]
    ga = jnp.where(keep, nn(v, gh) + nn(v, gl) + gd, 0.0)
    gab = ga.astype(BF)
    bh, bl = split(bs[b])
    gqf = nn(bh, gh) + nn(bh, gl) + nn(bl, gh) + norm * gd + nn(kf, gab)
    gk = nt(qf, gab)
    th, tl = split(gqf * sq)
    return nn(th, q) + nn(tl, q), back, backn, gk


def late_pass(vts, ks, sgs, gks, bks, bkn, unroll=1):
    zero = jnp.zeros((HD, HD), F32)

    def late(i, carry):
        st, nm, gwk = carry
        b = NB - 1 - i
        sh, sl = split(st)
        vt = vts[b]
        gk = nn(sh, vt) + nn(sl, vt) + nm[:, :1] + gks[b]
        th, tl = split(gk * sgs[b])
        k = ks[b]
        return (st + bks[b], nm + bkn[b], gwk + nn(th, k) + nn(tl, k))

    return lax.fori_loop(0, NB, late, (zero, zero, zero), unroll=unroll)[2]


def own_pass(c, qa, ls, accs, wqt, ks, vs, vts, kfs, bs, bst, bn, gks, bks, bkn):
    zero = jnp.zeros((HD, HD), F32)

    def slot(j, gwq):
        o = (c + j) % 2
        b = 2 * j + o
        teacher = (accs[j] / jnp.sum(ls[j], axis=1, keepdims=True)).astype(BF).astype(F32)
        g, back, backn, gk = own_block(qa[j], b, teacher.T, wqt, ks, vs, vts, kfs, bs, bst, bn, NB * R)
        gks[b] = gk
        gks[2 * j + 1 - o] = jnp.zeros((HD, R), F32)
        bks[b] = back
        bks[2 * j + 1 - o] = zero
        bkn[b] = jnp.broadcast_to(backn, (HD, HD))
        bkn[2 * j + 1 - o] = zero
        return gwq + g

    return lax.fori_loop(0, NZ, slot, zero, unroll=2)


def kernel(
    q, kin, vin, wq, wk, out,
    kv, qa, qs, ms, ls, accs, ks, vs, vts, kfs, sgs, bs, bst, bn, gks, bks, bkn, part, other,
    ring_s, ring_r, pair_s, pair_r, core_s, core_r, q_s, q_r, own_sem, swap_s, swap_r, far_s, far_r, fc_s, fc_r,
):
    s = lax.axis_index("seq")
    p = lax.axis_index("head")
    z, c, u = s // 2, s % 2, p % 2
    pair = (s, p + 1 - 2 * u)
    core = (2 * z + 1 - c, p)

    def remote(src, dst, ss, rs, to):
        return pltpu.make_async_remote_copy(
            src_ref=src, dst_ref=dst, send_sem=ss, recv_sem=rs, device_id=to, device_id_type=MESH_ID
        )

    def z_of(i):
        return (z + NZ + (i + 1) // 2 * (1 - 2 * (i % 2))) % NZ

    def at(half, zi, par):
        return kv.at[half, 2 * zi + par]

    def ring(n, src, zi):
        return remote(src, at(u, zi, c), ring_s.at[n], ring_r.at[n], (2 * ((z + NZ - 1 + 2 * (n % 2)) % NZ) + c, p))

    def to_pair(i, half, zi):
        return remote(at(half, zi, c), at(half, zi, c), pair_s.at[i], pair_r.at[i], pair)

    def to_core(way, i, half, zi, par):
        return remote(at(half, zi, par), at(half, zi, par), core_s.at[way, i], core_r.at[way, i], core)

    def heads(h):
        return q.at[:, pl.ds(pl.multiple_of(h * HD, HD), HD)]

    def send_q(n):
        h = (2 * z + NZ - z_of(n)) % NZ
        return remote(heads(h), qa.at[z], q_s.at[n], q_r.at[n], (2 * h + (c + z) % 2, p))

    kv[u, s] = jnp.concatenate((kin[...], vin[...]), axis=0).astype(F32).T.astype(BF)

    barrier = pltpu.get_barrier_semaphore()
    for d in range(1, NB):
        pl.semaphore_signal(barrier, inc=1, device_id=((s + d) % NB, p), device_id_type=MESH_ID)
    pl.semaphore_signal(barrier, inc=1, device_id=pair, device_id_type=MESH_ID)

    ms[...] = jnp.full(ms.shape, -1e30, F32)
    ls[...] = jnp.zeros(ls.shape, F32)
    accs[...] = jnp.zeros(accs.shape, F32)
    wqt = wq[z].astype(F32).T.astype(BF)
    wkt = wk[z].astype(F32).T.astype(BF)
    pl.semaphore_wait(barrier, NB)

    ring(1, at(u, z, c), z).start()
    ring(2, at(u, z, c), z).start()
    to_pair(0, u, z).start()
    to_core(0, 0, u, z, c).start()
    stay = pltpu.make_async_copy(heads(z), qa.at[z], own_sem)
    cross = remote(heads(z), qa.at[z], q_s.at[0], q_r.at[0], core)

    @pl.when(z % 2 == 0)
    def _():
        stay.start()

    @pl.when(z % 2 == 1)
    def _():
        cross.start()

    send_q(1).start()
    send_q(2).start()

    @pl.when(z % 2 == 0)
    def _():
        stay.wait()

    @pl.when(z % 2 == 1)
    def _():
        cross.wait()

    def step(i, x):
        zi = z_of(i)

        @pl.when(i < NZ - 1)
        def _():
            zn = z_of(i + 1)
            ring(i + 1, at(u, zn, c), zn).wait_recv()

            @pl.when(i + 3 < NZ)
            def _():
                ring(i + 3, at(u, zn, c), zn).start()

            to_pair(i + 1, u, zn).start()
            to_core(0, i + 1, u, zn, c).start()

        @pl.when(i + 3 < NZ)
        def _():
            send_q(i + 3).start()

        to_pair(i, 1 - u, zi).wait_recv()
        to_core(1, i, 1 - u, zi, c).start()
        to_core(0, i, u, zi, 1 - c).wait_recv()
        to_core(1, i, 1 - u, zi, 1 - c).wait_recv()

        @pl.when(i > 0)
        def _():
            remote(qa.at[zi], qa.at[zi], q_s.at[i], q_r.at[i], core).wait_recv()

        for e in range(2):
            prepare_block(2 * zi + e, kv, wkt, ks, vs, vts, kfs, sgs, bs, bst, bn)
        qs[zi] = (qa[zi].astype(F32) * (HD**-0.5 * LOG2E)).astype(BF)
        attend(zi, zi, (c + zi) % 2 * R, qs, ks, vs, ms, ls, accs)

        def item(t, y):
            zt = z_of(t)
            attend(jnp.maximum(zi, zt), jnp.minimum(zi, zt), None, qs, ks, vs, ms, ls, accs)
            return y

        lax.fori_loop(0, i, item, 0)
        return x

    lax.fori_loop(0, NZ, step, 0)
    prefix(bs, bst, bn)
    gwq = own_pass(c, qa, ls, accs, wqt, ks, vs, vts, kfs, bs, bst, bn, gks, bks, bkn)
    part[0] = gwq.T
    part[1] = late_pass(vts, ks, sgs, gks, bks, bkn, 4).T

    def drain(i, x):
        to_pair(i, u, z).wait_send()
        to_core(0, i, u, z, c).wait_send()
        to_core(1, i, u, z, c).wait_send()

        @pl.when(i > 0)
        def _():
            ring(i, at(u, z, c), z).wait_send()
            send_q(i).wait_send()

        return x

    lax.fori_loop(0, NZ, drain, 0)

    swap = remote(part.at[1 - c], other, swap_s, swap_r, core)
    swap.start()
    swap.wait()
    out[c, z] = (part[c] + other[...]).astype(BF)
    far = []
    for d in (1, 7, 2, 6, 3, 5, 4):
        far.append(remote(out.at[c, z], out.at[c, z], far_s.at[d], far_r.at[d], (2 * ((z + d) % NZ) + c, p)))
        far[-1].start()
    for d in (0, 1, 7, 2, 6, 3, 5, 4):
        got = out.at[c, (z + NZ - d) % NZ]
        if d:
            remote(got, got, far_s.at[d], far_r.at[d], core).wait_recv()
        far.append(remote(got, got, fc_s.at[d], fc_r.at[d], core))
        far[-1].start()
    for d in range(NZ):
        got = out.at[1 - c, (z + NZ - d) % NZ]
        remote(got, got, fc_s.at[d], fc_r.at[d], core).wait_recv()
    for copy in far:
        copy.wait_send()


def body(queries, keys, values, feat_q, feat_k):
    dma = pltpu.SemaphoreType.DMA
    vmem = pltpu.VMEM
    out = pl.pallas_call(
        kernel,
        out_shape=jax.ShapeDtypeStruct((2, NZ, HD, HD), BF),
        in_specs=[pl.BlockSpec(memory_space=pltpu.VMEM)] * 5,
        out_specs=pl.BlockSpec(memory_space=pltpu.VMEM),
        scratch_shapes=[
            vmem((2, NB, R, HD), BF),
            vmem((NZ, R, HD), BF),
            vmem((NZ, R, HD), BF),
            vmem((NZ, R, HD), F32),
            vmem((NZ, R, HD), F32),
            vmem((NZ, R, HD), F32),
            vmem((NB, R, HD), BF),
            vmem((NB, R, HD), BF),
            vmem((NB, HD, R), BF),
            vmem((NB, HD, R), BF),
            vmem((NB, HD, R), F32),
            vmem((NB, HD, HD), F32),
            vmem((NB, HD, HD), F32),
            vmem((NB, HD, HD), F32),
            vmem((NB, HD, R), F32),
            vmem((NB, HD, HD), F32),
            vmem((NB, HD, HD), F32),
            vmem((2, HD, HD), F32),
            vmem((HD, HD), F32),
            dma((NZ,)), dma((NZ,)), dma((NZ,)), dma((NZ,)), dma((2, NZ)), dma((2, NZ)), dma((NZ,)), dma((NZ,)),
            dma, dma, dma, dma((NZ,)), dma((NZ,)), dma((NZ,)), dma((NZ,)),
        ],
        compiler_params=pltpu.CompilerParams(collective_id=0, has_side_effects=True, vmem_limit_bytes=60000 * 1024),
    )(queries, keys.T, values.T, feat_q, feat_k)
    return out[0].astype(F32), out[1].astype(F32)


def solution(mesh):
    return jax.shard_map(
        body,
        mesh=mesh,
        in_specs=(P("seq", "head"), P("seq", "head"), P("seq", "head"), P("head", None, None), P("head", None, None)),
        out_specs=(P("head", None, None), P("head", None, None)),
        check_vma=False,
    )
```

```python
import jax
import jax.numpy as jnp
from jax import lax
from jax.experimental import pallas as pl
from jax.experimental.pallas import tpu as pltpu
from jax.sharding import PartitionSpec as P

BF = jnp.bfloat16
F32 = jnp.float32
R = 384
NB = 16
NZ = NB // 2
HD = 128
G = 2
RG = R // G
LOG2E = 1.4426950408889634


def nn(a, b):
    return lax.dot_general(a, b, (((1,), (0,)), ((), ())), preferred_element_type=F32)


def nt(a, b):
    return lax.dot_general(a, b, (((1,), (1,)), ((), ())), preferred_element_type=F32)


def tn(a, b):
    return lax.dot_general(a, b, (((0,), (0,)), ((), ())), preferred_element_type=F32)


def soft(v):
    e = jnp.exp(-jnp.abs(v))
    feat = jnp.maximum(v, 0.0) + jnp.log1p(e)
    gate = jnp.where(v >= 0.0, 1.0, e) / (1.0 + e)
    return feat.astype(BF), gate


def prepare_block(b, kv, wkt, ks, vs, vts, kfs, sgs, bs):
    lane = lax.broadcasted_iota(jnp.int32, (R, HD), 1)
    x0 = kv[0, b].astype(F32)
    x1 = kv[1, b].astype(F32)
    k = jnp.where(lane < 64, x0, pltpu.roll(x1, 64, 1)).astype(BF)
    vf = jnp.where(lane < 64, pltpu.roll(x0, 64, 1), x1)
    v = vf.astype(BF)
    ks[b] = k
    vs[b] = v
    vts[b] = vf.T.astype(BF)
    kf, sg = soft(nt(wkt, k))
    kfs[b] = kf
    sgs[b] = sg
    bs[b] = nn(kf, jnp.concatenate((v, jnp.ones((R, HD), BF)), axis=1))


def prefix(bs):
    def step(b, run):
        nxt = run + bs[b]
        bs[b] = run
        return nxt

    lax.fori_loop(0, NB, step, jnp.zeros((HD, 2 * HD), F32), unroll=2)


def score(slot, pair, qs, ks):
    k = ks[pl.ds(2 * pair, 2)].reshape(2 * R, HD)
    return [nt(qs[slot, g * RG : (g + 1) * RG], k) for g in range(G)]


def weigh(scores, slot, pair, shift, vs, ms, ls, accs):
    v = vs[pl.ds(2 * pair, 2)].reshape(2 * R, HD)
    for g in range(G):
        rows = slice(g * RG, (g + 1) * RG)
        s = scores[g]
        if shift is not None:
            dif = lax.broadcasted_iota(jnp.int32, s.shape, 1) - lax.broadcasted_iota(jnp.int32, s.shape, 0)
            s = jnp.where(dif <= shift + g * RG, s, -1e30)
        m = ms[slot, rows]
        mn = jnp.maximum(m, jnp.max(s, axis=1, keepdims=True))
        ms[slot, rows] = mn
        p = jnp.exp2(s - jnp.concatenate([mn] * (2 * R // HD), axis=1))
        a = jnp.exp2(m - mn)
        part = p[:, :HD]
        for t in range(1, 2 * R // HD):
            part = part + p[:, t * HD : (t + 1) * HD]
        ls[slot, rows] = ls[slot, rows] * a + part
        accs[slot, rows] = accs[slot, rows] * a + nn(p.astype(BF), v)


def attend(items, qs, ks, vs, ms, ls, accs):
    scores = [score(slot, pair, qs, ks) for slot, pair, _ in items]
    for sc, (slot, pair, shift) in zip(scores, items):
        weigh(sc, slot, pair, shift, vs, ms, ls, accs)


def own_block(q, b, teacher, wqt, vs, vts, kfs, bs):
    qf, sq = soft(nt(wqt, q))
    kf = kfs[b]
    row = lax.broadcasted_iota(jnp.int32, (R, R), 0)
    col = lax.broadcasted_iota(jnp.int32, (R, R), 1)
    keep = row <= col
    aff = jnp.where(keep, tn(kf, qf), 0.0)
    state = bs[b, :, :HD].astype(BF)
    norm = bs[b, :, HD : HD + 1]
    num = tn(state, qf) + nn(vts[b], aff.astype(BF))
    den = jnp.sum(norm * qf.astype(F32), axis=0, keepdims=True) + jnp.sum(aff, axis=0, keepdims=True)
    inv = 1.0 / den
    student = num * inv
    go = (student - teacher) * (2.0 / (NB * R))
    gn = go * inv
    gd = -jnp.sum(go * student, axis=0, keepdims=True) * inv
    gh = gn.astype(BF)
    back = nt(qf, gh)
    backn = jnp.sum(qf.astype(F32) * gd, axis=1, keepdims=True)
    ga = jnp.where(keep, nn(vs[b], gh) + gd, 0.0).astype(BF)
    gqf = nn(state, gh) + norm * gd + nn(kf, ga)
    gk = nt(qf, ga)
    return nn((gqf * sq).astype(BF), q), back, backn, gk


def late_pass(first, last, start, vts, ks, sgs, gks, bks, bkn):
    def late(i, carry):
        st, nm, gwk = carry
        b = NB - 1 - i
        gk = nn(st.astype(BF), vts[b]) + nm[:, :1] + gks[b]
        return (st + bks[b], nm + bkn[b], gwk + nn((gk * sgs[b]).astype(BF), ks[b]))

    return lax.fori_loop(first, last, late, start, unroll=4)


def own_pass(c, qa, ls, accs, wqt, vs, vts, kfs, bs, gks, bks, bkn):
    zero = jnp.zeros((HD, HD), F32)

    def slot(j, gwq):
        o = (c + j) % 2
        b = 2 * j + o
        teacher = (accs[j] / jnp.sum(ls[j], axis=1, keepdims=True)).astype(BF).astype(F32)
        g, back, backn, gk = own_block(qa[j], b, teacher.T, wqt, vs, vts, kfs, bs)
        gks[b] = gk
        bks[b] = back
        bkn[b] = jnp.broadcast_to(backn, (HD, HD))
        rest = 2 * j + 1 - o
        gks[rest] = jnp.zeros((HD, R), F32)
        bks[rest] = zero
        bkn[rest] = zero
        return gwq + g

    return lax.fori_loop(0, NZ, slot, zero, unroll=2)


MESH_ID = pl.DeviceIdType.MESH
AWAY = (1, 7, 2, 6, 3, 5, 4)
HALF = HD // 2


def kernel(
    q_hbm, k_hbm, v_hbm, wq_hbm, wk_hbm, out,
    q, kin, vin, wq, wk, kv, qa, qs, ms, ls, accs, ks, vs, vts, kfs, sgs, bs, gks, bks, bkn, part, other,
    load, ring_s, ring_r, pair_s, pair_r, core_s, core_r, q_s, q_r, own_sem, swap_s, swap_r, far_s, far_r, fc_s, fc_r,
):
    s = lax.axis_index("seq")
    p = lax.axis_index("head")
    z, c, u = s // 2, s % 2, p % 2
    pair = (s, p + 1 - 2 * u)
    core = (2 * z + 1 - c, p)

    def remote(src, dst, ss, rs, to):
        return pltpu.make_async_remote_copy(
            src_ref=src, dst_ref=dst, send_sem=ss, recv_sem=rs, device_id=to, device_id_type=MESH_ID
        )

    def z_of(i):
        return (z + NZ + (i + 1) // 2 * (1 - 2 * (i % 2))) % NZ

    def at(half, zi, par):
        return kv.at[half, 2 * zi + par]

    def ring(n, src, zi):
        return remote(src, at(u, zi, c), ring_s.at[n], ring_r.at[n], (2 * ((z + NZ - 1 + 2 * (n % 2)) % NZ) + c, p))

    def to_pair(i, half, zi):
        return remote(at(half, zi, c), at(half, zi, c), pair_s.at[i], pair_r.at[i], pair)

    def to_core(way, i, half, zi, par):
        return remote(at(half, zi, par), at(half, zi, par), core_s.at[way, i], core_r.at[way, i], core)

    def heads(h):
        return q.at[:, pl.ds(pl.multiple_of(h * HD, HD), HD)]

    def send_q(n):
        h = (2 * z + NZ - z_of(n)) % NZ
        return remote(heads(h), qa.at[z], q_s.at[n], q_r.at[n], (2 * h + (c + z) % 2, p))

    barrier = pltpu.get_barrier_semaphore()
    for d in range(1, NB):
        pl.semaphore_signal(barrier, inc=1, device_id=((s + d) % NB, p), device_id_type=MESH_ID)
    pl.semaphore_signal(barrier, inc=1, device_id=pair, device_id_type=MESH_ID)

    loads = [
        pltpu.make_async_copy(src, dst, load.at[n])
        for n, (src, dst) in enumerate(
            ((k_hbm, kin), (v_hbm, vin), (wq_hbm.at[z], wq), (wk_hbm.at[z], wk), (q_hbm, q))
        )
    ]
    for copy in loads:
        copy.start()
    ms[...] = jnp.full(ms.shape, -1e30, F32)
    ls[...] = jnp.zeros(ls.shape, F32)
    accs[...] = jnp.zeros(accs.shape, F32)
    for copy in loads:
        copy.wait()
    kv[u, s] = jnp.concatenate((kin[...], vin[...]), axis=0).astype(F32).T.astype(BF)
    wqt = wq[...].astype(F32).T.astype(BF)
    wkt = wk[...].astype(F32).T.astype(BF)
    pl.semaphore_wait(barrier, NB)

    ring(1, at(u, z, c), z).start()
    ring(2, at(u, z, c), z).start()
    to_pair(0, u, z).start()
    to_core(0, 0, u, z, c).start()
    stay = pltpu.make_async_copy(heads(z), qa.at[z], own_sem)
    cross = remote(heads(z), qa.at[z], q_s.at[0], q_r.at[0], core)

    @pl.when(z % 2 == 0)
    def _():
        stay.start()

    @pl.when(z % 2 == 1)
    def _():
        cross.start()

    send_q(1).start()
    send_q(2).start()

    @pl.when(z % 2 == 0)
    def _():
        stay.wait()

    @pl.when(z % 2 == 1)
    def _():
        cross.wait()

    state = (qs, ks, vs, ms, ls, accs)

    def cross_over(n):
        zn = z_of(n)
        to_pair(n, 1 - u, zn).wait_recv()
        to_core(1, n, 1 - u, zn, c).start()


    def advance(n):
        zn = z_of(n)
        ring(n, at(u, zn, c), zn).wait_recv()

        @pl.when(n + 2 < NZ)
        def _():
            ring(n + 2, at(u, zn, c), zn).start()

        to_pair(n, u, zn).start()
        to_core(0, n, u, zn, c).start()

        @pl.when(n + 2 < NZ)
        def _():
            send_q(n + 2).start()

    cross_over(0)

    def step(i, x):
        zi = z_of(i)

        @pl.when(i % 2 == 0)
        def _():
            advance(i + 1)

        @pl.when((i % 2 == 0) & (i + 2 < NZ))
        def _():
            advance(i + 2)

        to_core(0, i, u, zi, 1 - c).wait_recv()
        to_core(1, i, 1 - u, zi, 1 - c).wait_recv()

        @pl.when(i > 0)
        def _():
            remote(qa.at[zi], qa.at[zi], q_s.at[i], q_r.at[i], core).wait_recv()

        for e in range(2):
            prepare_block(2 * zi + e, kv, wkt, ks, vs, vts, kfs, sgs, bs)
        qs[zi] = (qa[zi].astype(F32) * (HD**-0.5 * LOG2E)).astype(BF)
        own = (zi, zi, (c + zi) % 2 * R)

        def item(t):
            zt = z_of(t)
            return jnp.maximum(zi, zt), jnp.minimum(zi, zt), None

        @pl.when(i + 1 < NZ)
        def _():
            cross_over(i + 1)

        @pl.when(i % 2 == 0)
        def _():
            attend((own,), *state)

        @pl.when(i % 2 == 1)
        def _():
            attend((item(i - 1), own), *state)

        def two(t, y):
            attend((item(2 * t), item(2 * t + 1)), *state)
            return y

        lax.fori_loop(0, i // 2, two, 0)
        return x

    lax.fori_loop(0, NZ, step, 0)
    prefix(bs)
    far = []

    def swap(g):
        return remote(part.at[g, 1 - c], other.at[g], swap_s.at[g], swap_r.at[g], core)

    def split_rows(g, value):
        part[g, 0] = value[:HALF]
        part[g, 1] = value[HALF:]

    def spread(g):
        out[g, z, c] = (part[g, c] + other[g]).astype(BF)
        for d in AWAY:
            mine = out.at[g, z, c]
            far.append(remote(mine, mine, far_s.at[g, d], far_r.at[g, d], (2 * ((z + d) % NZ) + c, p)))
            far[-1].start()

    def relay(g):
        for d in (0,) + AWAY:
            got = out.at[g, (z + NZ - d) % NZ, c]
            if d:
                remote(got, got, far_s.at[g, d], far_r.at[g, d], core).wait_recv()
            far.append(remote(got, got, fc_s.at[g, d], fc_r.at[g, d], core))
            far[-1].start()

    split_rows(0, own_pass(c, qa, ls, accs, wqt, vs, vts, kfs, bs, gks, bks, bkn).T)
    zero = jnp.zeros((HD, HD), F32)
    half = late_pass(0, NZ, (zero, zero, zero), vts, ks, sgs, gks, bks, bkn)
    swap(0).start()
    swap(0).wait()
    spread(0)
    split_rows(1, late_pass(NZ, NB, half, vts, ks, sgs, gks, bks, bkn)[2].T)

    def drain(i, x):
        to_pair(i, u, z).wait_send()
        to_core(0, i, u, z, c).wait_send()
        to_core(1, i, u, z, c).wait_send()

        @pl.when(i > 0)
        def _():
            ring(i, at(u, z, c), z).wait_send()
            send_q(i).wait_send()

        return x

    lax.fori_loop(0, NZ, drain, 0)
    swap(1).start()
    swap(1).wait()
    spread(1)
    relay(0)
    relay(1)
    for g in range(2):
        for d in range(NZ):
            got = out.at[g, (z + NZ - d) % NZ, 1 - c]
            remote(got, got, fc_s.at[g, d], fc_r.at[g, d], core).wait_recv()
    for copy in far:
        copy.wait_send()


def body(queries, keys, values, feat_q, feat_k):
    dma = pltpu.SemaphoreType.DMA
    vmem = pltpu.VMEM
    out = pl.pallas_call(
        kernel,
        out_shape=jax.ShapeDtypeStruct((2, NZ, 2, HALF, HD), BF),
        in_specs=[pl.BlockSpec(memory_space=pl.ANY)] * 5,
        out_specs=pl.BlockSpec(memory_space=pltpu.VMEM),
        scratch_shapes=[
            vmem((R, NZ * HD), BF),
            vmem((HALF, R), BF),
            vmem((HALF, R), BF),
            vmem((HD, HD), BF),
            vmem((HD, HD), BF),
            vmem((2, NB, R, HD), BF),
            vmem((NZ, R, HD), BF),
            vmem((NZ, R, HD), BF),
            vmem((NZ, R, HD), F32),
            vmem((NZ, R, HD), F32),
            vmem((NZ, R, HD), F32),
            vmem((NB, R, HD), BF),
            vmem((NB, R, HD), BF),
            vmem((NB, HD, R), BF),
            vmem((NB, HD, R), BF),
            vmem((NB, HD, R), F32),
            vmem((NB, HD, 2 * HD), F32),
            vmem((NB, HD, R), F32),
            vmem((NB, HD, HD), F32),
            vmem((NB, HD, HD), F32),
            vmem((2, 2, HALF, HD), F32),
            vmem((2, HALF, HD), F32),
            dma((5,)), dma((NZ,)), dma((NZ,)), dma((NZ,)), dma((NZ,)), dma((2, NZ)), dma((2, NZ)), dma((NZ,)), dma((NZ,)),
            dma, dma((2,)), dma((2,)), dma((2, NZ)), dma((2, NZ)), dma((2, NZ)), dma((2, NZ)),
        ],
        compiler_params=pltpu.CompilerParams(collective_id=0, has_side_effects=True, vmem_limit_bytes=60000 * 1024),
    )(queries, keys.T, values.T, feat_q, feat_k)
    out = out.reshape(2, NZ, HD, HD)
    return out[0].astype(F32), out[1].astype(F32)


def solution(mesh):
    return jax.shard_map(
        body,
        mesh=mesh,
        in_specs=(P("seq", "head"), P("seq", "head"), P("seq", "head"), P("head", None, None), P("head", None, None)),
        out_specs=(P("head", None, None), P("head", None, None)),
        check_vma=False,
    )
```

```python
import jax
import jax.numpy as jnp
from jax import lax
from jax.experimental import pallas as pl
from jax.experimental.pallas import tpu as pltpu
from jax.sharding import PartitionSpec as P

BF = jnp.bfloat16
F32 = jnp.float32
R = 384
NB = 16
NZ = NB // 2
HD = 128
G = 3
RG = R // G
LOG2E = 1.4426950408889634


def nn(a, b):
    return lax.dot_general(a, b, (((1,), (0,)), ((), ())), preferred_element_type=F32)


def nt(a, b):
    return lax.dot_general(a, b, (((1,), (1,)), ((), ())), preferred_element_type=F32)


def tn(a, b):
    return lax.dot_general(a, b, (((0,), (0,)), ((), ())), preferred_element_type=F32)


def soft(v):
    e = jnp.exp(-jnp.abs(v))
    low = jnp.where(e < 1e-3, e - (0.5 * e) * e, jnp.log(1.0 + e))
    feat = jnp.maximum(v, 0.0) + low
    return feat.astype(BF), jnp.exp(v - feat)


def prepare_block(b, kv, wkt, ks, vs, vts, kfs, sgs, bs):
    lane = lax.broadcasted_iota(jnp.int32, (R, HD), 1)
    x0 = kv[0, b].astype(F32)
    x1 = kv[1, b].astype(F32)
    k = jnp.where(lane < 64, x0, pltpu.roll(x1, 64, 1)).astype(BF)
    vf = jnp.where(lane < 64, pltpu.roll(x0, 64, 1), x1)
    v = vf.astype(BF)
    ks[b] = k
    vs[b] = v
    pre = nt(wkt, k)
    yield
    vts[b] = vf.T.astype(BF)
    yield
    kf, sg = soft(pre)
    kfs[b] = kf
    sgs[b] = sg
    yield
    bs[b] = nn(kf, jnp.concatenate((v, jnp.ones((R, HD), BF)), axis=1))
    yield


def prepare_pair(zi, *refs):
    runs = [prepare_block(2 * zi + e, *refs) for e in range(2)]
    for _ in range(4):
        for run in runs:
            next(run)


def prefix(bs):
    def step(b, run):
        nxt = run + bs[b]
        bs[b] = run
        return nxt

    lax.fori_loop(0, NB, step, jnp.zeros((HD, 2 * HD), F32), unroll=2)


def weigh(g, s, slot, pair, shift, vs, ms, ls, accs):
    rows = slice(g * RG, (g + 1) * RG)
    if shift is not None:
        dif = lax.broadcasted_iota(jnp.int32, s.shape, 1) - lax.broadcasted_iota(jnp.int32, s.shape, 0)
        s = jnp.where(dif <= shift + g * RG, s, -1e30)
    m = ms[slot, rows]
    mn = jnp.maximum(m, jnp.max(s, axis=1, keepdims=True))
    ms[slot, rows] = mn
    yield
    p = jnp.exp2(s - jnp.concatenate([mn] * (2 * R // HD), axis=1))
    a = jnp.exp2(m - mn)
    part = p[:, :HD]
    for t in range(1, 2 * R // HD):
        part = part + p[:, t * HD : (t + 1) * HD]
    ls[slot, rows] = ls[slot, rows] * a + part
    yield
    accs[slot, rows] = accs[slot, rows] * a + nn(p.astype(BF), vs[pl.ds(2 * pair, 2)].reshape(2 * R, HD))
    yield


def attend(items, qs, ks, vs, ms, ls, accs):
    k_of = [ks[pl.ds(2 * pair, 2)].reshape(2 * R, HD) for _, pair, _ in items]
    runs = []
    ahead = [(n, g) for n in range(len(items)) for g in range(G)]
    for t in range(len(ahead) + 3):
        if t < len(ahead):
            n, g = ahead[t]
            sc = nt(qs[items[n][0], g * RG : (g + 1) * RG], k_of[n])
        for run in runs[max(0, t - 3) : t]:
            next(run)
        if t < len(ahead):
            runs.append(weigh(g, sc, *items[n], vs, ms, ls, accs))


def own_block(q, b, teacher, wqt, vs, vts, kfs, bs):
    pre = nt(wqt, q)
    yield
    qf, sq = soft(pre)
    kf = kfs[b]
    yield
    row = lax.broadcasted_iota(jnp.int32, (R, R), 0)
    col = lax.broadcasted_iota(jnp.int32, (R, R), 1)
    keep = row <= col
    aff = tn(kf, qf)
    yield
    aff = jnp.where(keep, aff, 0.0)
    yield
    state = bs[b, :, :HD].astype(BF)
    norm = bs[b, :, HD : HD + 1]
    num = tn(state, qf) + nn(vts[b], aff.astype(BF))
    yield
    den = jnp.sum(norm * qf.astype(F32), axis=0, keepdims=True) + jnp.sum(aff, axis=0, keepdims=True)
    inv = 1.0 / den
    student = num * inv
    go = (student - teacher) * (2.0 / (NB * R))
    gn = go * inv
    gd = -jnp.sum(go * student, axis=0, keepdims=True) * inv
    gh = gn.astype(BF)
    yield
    back = nt(qf, gh)
    backn = jnp.sum(qf.astype(F32) * gd, axis=1, keepdims=True)
    yield
    ga = nn(vs[b], gh)
    yield
    ga = jnp.where(keep, ga + gd, 0.0).astype(BF)
    yield
    gqf = nn(state, gh) + norm * gd + nn(kf, ga)
    gk = nt(qf, ga)
    yield
    yield nn((gqf * sq).astype(BF), q), back, backn, gk


def late_pass(first, last, start, vts, ks, sgs, gks, bks, bkn):
    def late(i, carry):
        st, nm, gwk = carry
        b = NB - 1 - i
        gk = nn(st.astype(BF), vts[b]) + nm[:, :1] + gks[b]
        return (st + bks[b], nm + bkn[b], gwk + nn((gk * sgs[b]).astype(BF), ks[b]))

    return lax.fori_loop(first, last, late, start, unroll=4)


def own_pass(c, qa, ls, accs, wqt, vs, vts, kfs, bs, gks, bks, bkn):
    zero = jnp.zeros((HD, HD), F32)

    def slots(i, gwq):
        js = (2 * i, 2 * i + 1)
        blocks = [2 * j + (c + j) % 2 for j in js]
        teachers = [(accs[j] / jnp.sum(ls[j], axis=1, keepdims=True)).astype(BF).astype(F32).T for j in js]
        runs = [own_block(qa[j], b, t, wqt, vs, vts, kfs, bs) for j, b, t in zip(js, blocks, teachers)]
        done = [None, None]
        while done[1] is None:
            done = [next(run) for run in runs]
        for j, b, (g, back, backn, gk) in zip(js, blocks, done):
            gks[b] = gk
            bks[b] = back
            bkn[b] = jnp.broadcast_to(backn, (HD, HD))
            rest = 4 * j + 1 - b
            gks[rest] = jnp.zeros((HD, R), F32)
            bks[rest] = zero
            bkn[rest] = zero
            gwq = gwq + g
        return gwq

    return lax.fori_loop(0, NZ // 2, slots, zero)


MESH_ID = pl.DeviceIdType.MESH
AWAY = (1, 7, 2, 6, 3, 5, 4)
HALF = HD // 2


def kernel(
    q_hbm, k_hbm, v_hbm, wq_hbm, wk_hbm, out,
    q, kin, vin, wq, wk, kv, qa, qs, ms, ls, accs, ks, vs, vts, kfs, sgs, bs, gks, bks, bkn, part, other,
    load, ring_s, ring_r, pair_s, pair_r, core_s, core_r, q_s, q_r, own_sem, swap_s, swap_r, far_s, far_r, fc_s, fc_r,
):
    s = lax.axis_index("seq")
    p = lax.axis_index("head")
    z, c, u = s // 2, s % 2, p % 2
    pair = (s, p + 1 - 2 * u)
    core = (2 * z + 1 - c, p)

    def remote(src, dst, ss, rs, to):
        return pltpu.make_async_remote_copy(
            src_ref=src, dst_ref=dst, send_sem=ss, recv_sem=rs, device_id=to, device_id_type=MESH_ID
        )

    def z_of(i):
        return (z + NZ + (i + 1) // 2 * (1 - 2 * (i % 2))) % NZ

    def at(half, zi, par):
        return kv.at[half, 2 * zi + par]

    def ring(n, src, zi):
        return remote(src, at(u, zi, c), ring_s.at[n], ring_r.at[n], (2 * ((z + NZ - 1 + 2 * (n % 2)) % NZ) + c, p))

    def to_pair(i, half, zi):
        return remote(at(half, zi, c), at(half, zi, c), pair_s.at[i], pair_r.at[i], pair)

    def to_core(way, i, half, zi, par):
        return remote(at(half, zi, par), at(half, zi, par), core_s.at[way, i], core_r.at[way, i], core)

    def heads(h):
        return q.at[:, pl.ds(pl.multiple_of(h * HD, HD), HD)]

    def send_q(n):
        h = (2 * z + NZ - z_of(n)) % NZ
        return remote(heads(h), qa.at[z], q_s.at[n], q_r.at[n], (2 * h + (c + z) % 2, p))

    barrier = pltpu.get_barrier_semaphore()
    for d in range(1, NB):
        pl.semaphore_signal(barrier, inc=1, device_id=((s + d) % NB, p), device_id_type=MESH_ID)
    pl.semaphore_signal(barrier, inc=1, device_id=pair, device_id_type=MESH_ID)

    loads = [
        pltpu.make_async_copy(src, dst, load.at[n])
        for n, (src, dst) in enumerate(
            ((k_hbm, kin), (v_hbm, vin), (wq_hbm.at[z], wq), (wk_hbm.at[z], wk), (q_hbm, q))
        )
    ]
    for copy in loads:
        copy.start()
    ms[...] = jnp.full(ms.shape, -1e30, F32)
    ls[...] = jnp.zeros(ls.shape, F32)
    accs[...] = jnp.zeros(accs.shape, F32)
    for copy in loads:
        copy.wait()
    kv[u, s] = jnp.concatenate((kin[...], vin[...]), axis=0).astype(F32).T.astype(BF)
    wqt = wq[...].astype(F32).T.astype(BF)
    wkt = wk[...].astype(F32).T.astype(BF)
    pl.semaphore_wait(barrier, NB)

    ring(1, at(u, z, c), z).start()
    ring(2, at(u, z, c), z).start()
    to_pair(0, u, z).start()
    to_core(0, 0, u, z, c).start()
    stay = pltpu.make_async_copy(heads(z), qa.at[z], own_sem)
    cross = remote(heads(z), qa.at[z], q_s.at[0], q_r.at[0], core)

    @pl.when(z % 2 == 0)
    def _():
        stay.start()

    @pl.when(z % 2 == 1)
    def _():
        cross.start()

    send_q(1).start()
    send_q(2).start()

    @pl.when(z % 2 == 0)
    def _():
        stay.wait()

    @pl.when(z % 2 == 1)
    def _():
        cross.wait()

    state = (qs, ks, vs, ms, ls, accs)

    def advance(n):
        zn = z_of(n)
        ring(n, at(u, zn, c), zn).wait_recv()

        @pl.when(n + 2 < NZ)
        def _():
            ring(n + 2, at(u, zn, c), zn).start()

        to_pair(n, u, zn).start()
        to_core(0, n, u, zn, c).start()

        @pl.when(n + 2 < NZ)
        def _():
            send_q(n + 2).start()

    def step(i, x):
        zi = z_of(i)

        @pl.when(i % 2 == 0)
        def _():
            advance(i + 1)

        @pl.when((i % 2 == 0) & (i + 2 < NZ))
        def _():
            advance(i + 2)

        to_pair(i, 1 - u, zi).wait_recv()
        to_core(1, i, 1 - u, zi, c).start()
        to_core(0, i, u, zi, 1 - c).wait_recv()
        to_core(1, i, 1 - u, zi, 1 - c).wait_recv()

        @pl.when(i > 0)
        def _():
            remote(qa.at[zi], qa.at[zi], q_s.at[i], q_r.at[i], core).wait_recv()

        prepare_pair(zi, kv, wkt, ks, vs, vts, kfs, sgs, bs)
        qs[zi] = (qa[zi].astype(F32) * (HD**-0.5 * LOG2E)).astype(BF)
        own = (zi, zi, (c + zi) % 2 * R)

        def item(t):
            zt = z_of(t)
            return jnp.maximum(zi, zt), jnp.minimum(zi, zt), None

        @pl.when(i % 2 == 0)
        def _():
            attend((own,), *state)

        @pl.when(i % 2 == 1)
        def _():
            attend((item(i - 1), own), *state)

        def two(t, y):
            attend((item(2 * t), item(2 * t + 1)), *state)
            return y

        lax.fori_loop(0, i // 2, two, 0)
        return x

    lax.fori_loop(0, NZ, step, 0)
    prefix(bs)
    far = []

    def swap(g):
        return remote(part.at[g, 1 - c], other.at[g], swap_s.at[g], swap_r.at[g], core)

    def split_rows(g, value):
        part[g, 0] = value[:HALF]
        part[g, 1] = value[HALF:]

    def spread(g):
        out[g, z, c] = (part[g, c] + other[g]).astype(BF)
        for d in AWAY:
            mine = out.at[g, z, c]
            far.append(remote(mine, mine, far_s.at[g, d], far_r.at[g, d], (2 * ((z + d) % NZ) + c, p)))
            far[-1].start()

    def relay(g):
        for d in (0,) + AWAY:
            got = out.at[g, (z + NZ - d) % NZ, c]
            if d:
                remote(got, got, far_s.at[g, d], far_r.at[g, d], core).wait_recv()
            far.append(remote(got, got, fc_s.at[g, d], fc_r.at[g, d], core))
            far[-1].start()

    split_rows(0, own_pass(c, qa, ls, accs, wqt, vs, vts, kfs, bs, gks, bks, bkn).T)
    zero = jnp.zeros((HD, HD), F32)
    half = late_pass(0, NZ, (zero, zero, zero), vts, ks, sgs, gks, bks, bkn)
    swap(0).start()
    swap(0).wait()
    spread(0)
    split_rows(1, late_pass(NZ, NB, half, vts, ks, sgs, gks, bks, bkn)[2].T)

    def drain(i, x):
        to_pair(i, u, z).wait_send()
        to_core(0, i, u, z, c).wait_send()
        to_core(1, i, u, z, c).wait_send()

        @pl.when(i > 0)
        def _():
            ring(i, at(u, z, c), z).wait_send()
            send_q(i).wait_send()

        return x

    lax.fori_loop(0, NZ, drain, 0)
    swap(1).start()
    swap(1).wait()
    spread(1)
    relay(0)
    relay(1)
    for g in range(2):
        for d in range(NZ):
            got = out.at[g, (z + NZ - d) % NZ, 1 - c]
            remote(got, got, fc_s.at[g, d], fc_r.at[g, d], core).wait_recv()
    for copy in far:
        copy.wait_send()


def body(queries, keys, values, feat_q, feat_k):
    dma = pltpu.SemaphoreType.DMA
    vmem = pltpu.VMEM
    out = pl.pallas_call(
        kernel,
        out_shape=jax.ShapeDtypeStruct((2, NZ, 2, HALF, HD), BF),
        in_specs=[pl.BlockSpec(memory_space=pl.ANY)] * 5,
        out_specs=pl.BlockSpec(memory_space=pltpu.VMEM),
        scratch_shapes=[
            vmem((R, NZ * HD), BF),
            vmem((HALF, R), BF),
            vmem((HALF, R), BF),
            vmem((HD, HD), BF),
            vmem((HD, HD), BF),
            vmem((2, NB, R, HD), BF),
            vmem((NZ, R, HD), BF),
            vmem((NZ, R, HD), BF),
            vmem((NZ, R, HD), F32),
            vmem((NZ, R, HD), F32),
            vmem((NZ, R, HD), F32),
            vmem((NB, R, HD), BF),
            vmem((NB, R, HD), BF),
            vmem((NB, HD, R), BF),
            vmem((NB, HD, R), BF),
            vmem((NB, HD, R), F32),
            vmem((NB, HD, 2 * HD), F32),
            vmem((NB, HD, R), F32),
            vmem((NB, HD, HD), F32),
            vmem((NB, HD, HD), F32),
            vmem((2, 2, HALF, HD), F32),
            vmem((2, HALF, HD), F32),
            dma((5,)), dma((NZ,)), dma((NZ,)), dma((NZ,)), dma((NZ,)), dma((2, NZ)), dma((2, NZ)), dma((NZ,)), dma((NZ,)),
            dma, dma((2,)), dma((2,)), dma((2, NZ)), dma((2, NZ)), dma((2, NZ)), dma((2, NZ)),
        ],
        compiler_params=pltpu.CompilerParams(collective_id=0, has_side_effects=True, vmem_limit_bytes=60000 * 1024),
    )(queries, keys.T, values.T, feat_q, feat_k)
    out = out.reshape(2, NZ, HD, HD)
    return out[0].astype(F32), out[1].astype(F32)


def solution(mesh):
    return jax.shard_map(
        body,
        mesh=mesh,
        in_specs=(P("seq", "head"), P("seq", "head"), P("seq", "head"), P("head", None, None), P("head", None, None)),
        out_specs=(P("head", None, None), P("head", None, None)),
        check_vma=False,
    )
```

```python
import jax
import jax.numpy as jnp
from jax import lax
from jax.experimental import pallas as pl
from jax.experimental.pallas import tpu as pltpu
from jax.sharding import PartitionSpec as P

BF = jnp.bfloat16
F32 = jnp.float32
R = 384
NB = 16
NZ = NB // 2
HD = 128
G = 3
RG = R // G
LOG2E = 1.4426950408889634


def nn(a, b):
    return lax.dot_general(a, b, (((1,), (0,)), ((), ())), preferred_element_type=F32)


def nt(a, b):
    return lax.dot_general(a, b, (((1,), (1,)), ((), ())), preferred_element_type=F32)


def tn(a, b):
    return lax.dot_general(a, b, (((0,), (0,)), ((), ())), preferred_element_type=F32)


def soft(v):
    e = jnp.exp(-jnp.abs(v))
    low = jnp.where(e < 1e-3, e - (0.5 * e) * e, jnp.log(1.0 + e))
    feat = jnp.maximum(v, 0.0) + low
    return feat.astype(BF), jnp.exp(v - feat)


def prepare_block(b, kv, wkt, ks, vs, vts, kfs, sgs, bs):
    lane = lax.broadcasted_iota(jnp.int32, (R, HD), 1)
    x0 = kv[0, b].astype(F32)
    x1 = kv[1, b].astype(F32)
    k = jnp.where(lane < 64, x0, pltpu.roll(x1, 64, 1)).astype(BF)
    vf = jnp.where(lane < 64, pltpu.roll(x0, 64, 1), x1)
    v = vf.astype(BF)
    ks[b] = k
    vs[b] = v
    pre = nt(wkt, k)
    yield
    vts[b] = vf.T.astype(BF)
    yield
    kf, sg = soft(pre)
    kfs[b] = kf
    sgs[b] = sg
    yield
    bs[b] = nn(kf, jnp.concatenate((v, jnp.ones((R, HD), BF)), axis=1))
    yield


def prepare_pair(zi, *refs):
    runs = [prepare_block(2 * zi + e, *refs) for e in range(2)]
    for _ in range(4):
        for run in runs:
            next(run)


def prefix(bs):
    def step(b, run):
        nxt = run + bs[b]
        bs[b] = run
        return nxt

    lax.fori_loop(0, NB, step, jnp.zeros((HD, 2 * HD), F32), unroll=2)


def weigh(g, s, slot, pair, shift, vs, ms, ls, accs):
    rows = slice(g * RG, (g + 1) * RG)
    if shift is not None:
        dif = lax.broadcasted_iota(jnp.int32, s.shape, 1) - lax.broadcasted_iota(jnp.int32, s.shape, 0)
        s = jnp.where(dif <= shift + g * RG, s, -1e30)
    m = ms[slot, rows]
    mn = jnp.maximum(m, jnp.max(s, axis=1, keepdims=True))
    ms[slot, rows] = mn
    yield
    p = jnp.exp2(s - jnp.concatenate([mn] * (2 * R // HD), axis=1))
    a = jnp.exp2(m - mn)
    part = p[:, :HD]
    for t in range(1, 2 * R // HD):
        part = part + p[:, t * HD : (t + 1) * HD]
    ls[slot, rows] = ls[slot, rows] * a + part
    yield
    accs[slot, rows] = accs[slot, rows] * a + nn(p.astype(BF), vs[pl.ds(2 * pair, 2)].reshape(2 * R, HD))
    yield


def attend(items, qs, ks, vs, ms, ls, accs):
    k_of = [ks[pl.ds(2 * pair, 2)].reshape(2 * R, HD) for _, pair, _ in items]
    runs = []
    ahead = [(n, g) for n in range(len(items)) for g in range(G)]
    for t in range(len(ahead) + 3):
        if t < len(ahead):
            n, g = ahead[t]
            sc = nt(qs[items[n][0], g * RG : (g + 1) * RG], k_of[n])
        for run in runs[max(0, t - 3) : t]:
            next(run)
        if t < len(ahead):
            runs.append(weigh(g, sc, *items[n], vs, ms, ls, accs))


def front(j, c, qa, wqt, vts, kfs, qfs, sqs, mixs, afs):
    b = 2 * j + (c + j) % 2
    qf, sq = soft(nt(wqt, qa[j]))
    row = lax.broadcasted_iota(jnp.int32, (R, R), 0)
    col = lax.broadcasted_iota(jnp.int32, (R, R), 1)
    aff = jnp.where(row <= col, tn(kfs[b], qf), 0.0)
    qfs[j] = qf
    sqs[j] = sq
    mixs[j] = nn(vts[b], aff.astype(BF))
    afs[j] = jnp.broadcast_to(jnp.sum(aff, axis=0, keepdims=True), (8, R))


def own_block(j, q, b, teacher, vs, kfs, bs, qfs, sqs, mixs, afs):
    qf, sq, kf = qfs[j], sqs[j], kfs[b]
    row = lax.broadcasted_iota(jnp.int32, (R, R), 0)
    col = lax.broadcasted_iota(jnp.int32, (R, R), 1)
    keep = row <= col
    state = bs[b, :, :HD].astype(BF)
    norm = bs[b, :, HD : HD + 1]
    num = tn(state, qf) + mixs[j]
    yield
    den = jnp.sum(norm * qf.astype(F32), axis=0, keepdims=True) + afs[j, :1]
    inv = 1.0 / den
    student = num * inv
    go = (student - teacher) * (2.0 / (NB * R))
    gn = go * inv
    gd = -jnp.sum(go * student, axis=0, keepdims=True) * inv
    gh = gn.astype(BF)
    yield
    back = nt(qf, gh)
    backn = jnp.sum(qf.astype(F32) * gd, axis=1, keepdims=True)
    yield
    ga = nn(vs[b], gh)
    yield
    ga = jnp.where(keep, ga + gd, 0.0).astype(BF)
    yield
    gqf = nn(state, gh) + norm * gd + nn(kf, ga)
    gk = nt(qf, ga)
    yield
    yield nn((gqf * sq).astype(BF), q), back, backn, gk


def late_pass(first, last, start, vts, ks, sgs, gks, bks, bkn):
    def late(i, carry):
        st, nm, gwk = carry
        b = NB - 1 - i
        gk = nn(st.astype(BF), vts[b]) + nm[:, :1] + gks[b]
        return (st + bks[b], nm + bkn[b], gwk + nn((gk * sgs[b]).astype(BF), ks[b]))

    return lax.fori_loop(first, last, late, start, unroll=4)


def own_pass(c, qa, ls, accs, vs, kfs, bs, qfs, sqs, mixs, afs, gks, bks, bkn):
    zero = jnp.zeros((HD, HD), F32)

    def slots(i, gwq):
        js = (2 * i, 2 * i + 1)
        blocks = [2 * j + (c + j) % 2 for j in js]
        teachers = [(accs[j] / jnp.sum(ls[j], axis=1, keepdims=True)).astype(BF).astype(F32).T for j in js]
        runs = [own_block(j, qa[j], b, t, vs, kfs, bs, qfs, sqs, mixs, afs) for j, b, t in zip(js, blocks, teachers)]
        done = [None, None]
        while done[1] is None:
            done = [next(run) for run in runs]
        for j, b, (g, back, backn, gk) in zip(js, blocks, done):
            gks[b] = gk
            bks[b] = back
            bkn[b] = jnp.broadcast_to(backn, (HD, HD))
            rest = 4 * j + 1 - b
            gks[rest] = jnp.zeros((HD, R), F32)
            bks[rest] = zero
            bkn[rest] = zero
            gwq = gwq + g
        return gwq

    return lax.fori_loop(0, NZ // 2, slots, zero)


MESH_ID = pl.DeviceIdType.MESH
AWAY = (1, 7, 2, 6, 3, 5, 4)
HALF = HD // 2


def kernel(
    q_hbm, k_hbm, v_hbm, wq_hbm, wk_hbm, out,
    q, kin, vin, wq, wk, kv, qa, qs, ms, ls, accs, ks, vs, vts, kfs, sgs, bs, qfs, sqs, mixs, afs, gks, bks, bkn, part, other,
    load, ring_s, ring_r, pair_s, pair_r, core_s, core_r, q_s, q_r, own_sem, swap_s, swap_r, far_s, far_r, fc_s, fc_r,
):
    s = lax.axis_index("seq")
    p = lax.axis_index("head")
    z, c, u = s // 2, s % 2, p % 2
    pair = (s, p + 1 - 2 * u)
    core = (2 * z + 1 - c, p)

    def remote(src, dst, ss, rs, to):
        return pltpu.make_async_remote_copy(
            src_ref=src, dst_ref=dst, send_sem=ss, recv_sem=rs, device_id=to, device_id_type=MESH_ID
        )

    def z_of(i):
        return (z + NZ + (i + 1) // 2 * (1 - 2 * (i % 2))) % NZ

    def at(half, zi, par):
        return kv.at[half, 2 * zi + par]

    def ring(n, src, zi):
        return remote(src, at(u, zi, c), ring_s.at[n], ring_r.at[n], (2 * ((z + NZ - 1 + 2 * (n % 2)) % NZ) + c, p))

    def to_pair(i, half, zi):
        return remote(at(half, zi, c), at(half, zi, c), pair_s.at[i], pair_r.at[i], pair)

    def to_core(way, i, half, zi, par):
        return remote(at(half, zi, par), at(half, zi, par), core_s.at[way, i], core_r.at[way, i], core)

    def heads(h):
        return q.at[:, pl.ds(pl.multiple_of(h * HD, HD), HD)]

    def send_q(n):
        h = (2 * z + NZ - z_of(n)) % NZ
        return remote(heads(h), qa.at[z], q_s.at[n], q_r.at[n], (2 * h + (c + z) % 2, p))

    barrier = pltpu.get_barrier_semaphore()
    for d in range(1, NB):
        pl.semaphore_signal(barrier, inc=1, device_id=((s + d) % NB, p), device_id_type=MESH_ID)
    pl.semaphore_signal(barrier, inc=1, device_id=pair, device_id_type=MESH_ID)

    loads = [
        pltpu.make_async_copy(src, dst, load.at[n])
        for n, (src, dst) in enumerate(
            ((k_hbm, kin), (v_hbm, vin), (wq_hbm.at[z], wq), (wk_hbm.at[z], wk), (q_hbm, q))
        )
    ]
    for copy in loads:
        copy.start()
    ms[...] = jnp.full(ms.shape, -1e30, F32)
    ls[...] = jnp.zeros(ls.shape, F32)
    accs[...] = jnp.zeros(accs.shape, F32)
    for copy in loads:
        copy.wait()
    kv[u, s] = jnp.concatenate((kin[...], vin[...]), axis=0).astype(F32).T.astype(BF)
    wqt = wq[...].astype(F32).T.astype(BF)
    wkt = wk[...].astype(F32).T.astype(BF)
    pl.semaphore_wait(barrier, NB)

    ring(1, at(u, z, c), z).start()
    ring(2, at(u, z, c), z).start()
    to_pair(0, u, z).start()
    to_core(0, 0, u, z, c).start()
    stay = pltpu.make_async_copy(heads(z), qa.at[z], own_sem)
    cross = remote(heads(z), qa.at[z], q_s.at[0], q_r.at[0], core)

    @pl.when(z % 2 == 0)
    def _():
        stay.start()

    @pl.when(z % 2 == 1)
    def _():
        cross.start()

    send_q(1).start()
    send_q(2).start()

    @pl.when(z % 2 == 0)
    def _():
        stay.wait()

    @pl.when(z % 2 == 1)
    def _():
        cross.wait()

    state = (qs, ks, vs, ms, ls, accs)

    def advance(n):
        zn = z_of(n)
        ring(n, at(u, zn, c), zn).wait_recv()

        @pl.when(n + 2 < NZ)
        def _():
            ring(n + 2, at(u, zn, c), zn).start()

        to_pair(n, u, zn).start()
        to_core(0, n, u, zn, c).start()

        @pl.when(n + 2 < NZ)
        def _():
            send_q(n + 2).start()

    def step(i, x):
        zi = z_of(i)

        @pl.when(i % 2 == 0)
        def _():
            advance(i + 1)

        @pl.when((i % 2 == 0) & (i + 2 < NZ))
        def _():
            advance(i + 2)

        to_pair(i, 1 - u, zi).wait_recv()
        to_core(1, i, 1 - u, zi, c).start()

        @pl.when(i > 0)
        def _():
            front(z_of(i - 1), c, qa, wqt, vts, kfs, qfs, sqs, mixs, afs)

        to_core(0, i, u, zi, 1 - c).wait_recv()
        to_core(1, i, 1 - u, zi, 1 - c).wait_recv()

        @pl.when(i > 0)
        def _():
            remote(qa.at[zi], qa.at[zi], q_s.at[i], q_r.at[i], core).wait_recv()

        prepare_pair(zi, kv, wkt, ks, vs, vts, kfs, sgs, bs)
        qs[zi] = (qa[zi].astype(F32) * (HD**-0.5 * LOG2E)).astype(BF)
        own = (zi, zi, (c + zi) % 2 * R)

        def item(t):
            zt = z_of(t)
            return jnp.maximum(zi, zt), jnp.minimum(zi, zt), None

        @pl.when(i % 2 == 0)
        def _():
            attend((own,), *state)

        @pl.when(i % 2 == 1)
        def _():
            attend((item(i - 1), own), *state)

        def two(t, y):
            attend((item(2 * t), item(2 * t + 1)), *state)
            return y

        lax.fori_loop(0, i // 2, two, 0)
        return x

    lax.fori_loop(0, NZ, step, 0)
    front(z_of(NZ - 1), c, qa, wqt, vts, kfs, qfs, sqs, mixs, afs)
    prefix(bs)
    far = []

    def swap(g):
        return remote(part.at[g, 1 - c], other.at[g], swap_s.at[g], swap_r.at[g], core)

    def split_rows(g, value):
        part[g, 0] = value[:HALF]
        part[g, 1] = value[HALF:]

    def spread(g):
        out[g, z, c] = (part[g, c] + other[g]).astype(BF)
        for d in AWAY:
            mine = out.at[g, z, c]
            far.append(remote(mine, mine, far_s.at[g, d], far_r.at[g, d], (2 * ((z + d) % NZ) + c, p)))
            far[-1].start()

    def relay(g):
        for d in (0,) + AWAY:
            got = out.at[g, (z + NZ - d) % NZ, c]
            if d:
                remote(got, got, far_s.at[g, d], far_r.at[g, d], core).wait_recv()
            far.append(remote(got, got, fc_s.at[g, d], fc_r.at[g, d], core))
            far[-1].start()

    split_rows(0, own_pass(c, qa, ls, accs, vs, kfs, bs, qfs, sqs, mixs, afs, gks, bks, bkn).T)
    zero = jnp.zeros((HD, HD), F32)
    half = late_pass(0, NZ, (zero, zero, zero), vts, ks, sgs, gks, bks, bkn)
    swap(0).start()
    swap(0).wait()
    spread(0)
    split_rows(1, late_pass(NZ, NB, half, vts, ks, sgs, gks, bks, bkn)[2].T)

    def drain(i, x):
        to_pair(i, u, z).wait_send()
        to_core(0, i, u, z, c).wait_send()
        to_core(1, i, u, z, c).wait_send()

        @pl.when(i > 0)
        def _():
            ring(i, at(u, z, c), z).wait_send()
            send_q(i).wait_send()

        return x

    lax.fori_loop(0, NZ, drain, 0)
    swap(1).start()
    swap(1).wait()
    spread(1)
    relay(0)
    relay(1)
    for g in range(2):
        for d in range(NZ):
            got = out.at[g, (z + NZ - d) % NZ, 1 - c]
            remote(got, got, fc_s.at[g, d], fc_r.at[g, d], core).wait_recv()
    for copy in far:
        copy.wait_send()


def body(queries, keys, values, feat_q, feat_k):
    dma = pltpu.SemaphoreType.DMA
    vmem = pltpu.VMEM
    out = pl.pallas_call(
        kernel,
        out_shape=jax.ShapeDtypeStruct((2, NZ, 2, HALF, HD), BF),
        in_specs=[pl.BlockSpec(memory_space=pl.ANY)] * 5,
        out_specs=pl.BlockSpec(memory_space=pltpu.VMEM),
        scratch_shapes=[
            vmem((R, NZ * HD), BF),
            vmem((HALF, R), BF),
            vmem((HALF, R), BF),
            vmem((HD, HD), BF),
            vmem((HD, HD), BF),
            vmem((2, NB, R, HD), BF),
            vmem((NZ, R, HD), BF),
            vmem((NZ, R, HD), BF),
            vmem((NZ, R, HD), F32),
            vmem((NZ, R, HD), F32),
            vmem((NZ, R, HD), F32),
            vmem((NB, R, HD), BF),
            vmem((NB, R, HD), BF),
            vmem((NB, HD, R), BF),
            vmem((NB, HD, R), BF),
            vmem((NB, HD, R), F32),
            vmem((NB, HD, 2 * HD), F32),
            vmem((NZ, HD, R), BF),
            vmem((NZ, HD, R), F32),
            vmem((NZ, HD, R), F32),
            vmem((NZ, 8, R), F32),
            vmem((NB, HD, R), F32),
            vmem((NB, HD, HD), F32),
            vmem((NB, HD, HD), F32),
            vmem((2, 2, HALF, HD), F32),
            vmem((2, HALF, HD), F32),
            dma((5,)), dma((NZ,)), dma((NZ,)), dma((NZ,)), dma((NZ,)), dma((2, NZ)), dma((2, NZ)), dma((NZ,)), dma((NZ,)),
            dma, dma((2,)), dma((2,)), dma((2, NZ)), dma((2, NZ)), dma((2, NZ)), dma((2, NZ)),
        ],
        compiler_params=pltpu.CompilerParams(collective_id=0, has_side_effects=True, vmem_limit_bytes=60000 * 1024),
    )(queries, keys.T, values.T, feat_q, feat_k)
    out = out.reshape(2, NZ, HD, HD)
    return out[0].astype(F32), out[1].astype(F32)


def solution(mesh):
    return jax.shard_map(
        body,
        mesh=mesh,
        in_specs=(P("seq", "head"), P("seq", "head"), P("seq", "head"), P("head", None, None), P("head", None, None)),
        out_specs=(P("head", None, None), P("head", None, None)),
        check_vma=False,
    )
```
